32 devices in a mesh: row: 8 (over y, x, core), feat: 4 (over z).
Axes of the slice: x: 2, y: 2, z: 4, core: 2. Of those that a mesh axis runs over, the one named last changes fastest.
Arguments:
- bins: int32 [1024, 65536], P('feat', 'row'), may hold values from 0 to 255
- grads: bfloat16 [65536], P('row'), may hold values from -6 to 6
- hess: bfloat16 [65536], P('row'), may hold values from 0.049804688 to 1
- node: int32 [65536], P('row'), may hold values from 0 to 7
Outputs:
- shortfall: float32 [1024, 8, 256], P(('feat', 'row'))
- best: float32 [8], replicated
The draws below stay inside these ranges and needn't reach their ends.
All inputs are finite; a program needn't handle non-finite values.
Results may differ from the reference program's by a relative error of at most 0.0003.
Values sent between devices are 32-bit elements; how exact they have to be, the bound alone decides.
A program may use at most 64 MiB of HBM per device.

```python
import math
import jax
import jax.numpy as jnp
from jax import lax

FEATURES = 1024
BINS = 256
NODES = 8
ROWS = 65536


def plant(entries, key, smallest, largest):
    dims = entries.shape
    index_at = [jax.random.randint(jax.random.fold_in(key, axis), (), 0, dims[axis]) for axis in range(len(dims))]
    entries = entries.at[tuple(index_at)].set(smallest)
    longest = dims.index(max(dims))
    index_at[longest] = (index_at[longest] + 1) % dims[longest]
    return entries.at[tuple(index_at)].set(largest)


def block_levels(rng, shape, cuts, least, high):
    def one(axis_at, parts):
        steps = jax.random.uniform(jax.random.fold_in(jax.random.fold_in(rng, 6), axis_at), (parts,), jnp.float32, least / len(cuts), high / len(cuts))
        return jnp.repeat(jnp.exp(steps), shape[axis_at] // parts).reshape((-1,) + (1,) * (len(shape) - axis_at - 1))

    level = one(*cuts[0])
    for cut in cuts[1:]:
        level = level * one(*cut)
    return level


def scatter_about(stream_key, dims, spread, reach, split=(), held_as=jnp.bfloat16):
    loudness = block_levels(stream_key, dims, split, -0.22, 0.18) if split else 1.0
    result = jax.random.normal(stream_key, dims, jnp.float32) * spread * loudness
    return jnp.minimum(jnp.maximum(result, -reach), reach).astype(held_as)


def setup_inputs(seed: int = 0) -> dict:
    key_of = jax.random.split(jax.random.key(seed), 5)
    bins = plant(jax.random.randint(key_of[0], (FEATURES, ROWS), 0, BINS), jax.random.fold_in(key_of[0], 1), 0, BINS - 1).astype(jnp.int32)
    grads = scatter_about(key_of[1], (ROWS,), 1.0, 6.0, ((0, 8),))
    hess = jnp.clip(jnp.exp(math.log(1.0) - 2.9996462 * jax.random.uniform(key_of[2], (ROWS,), jnp.float32) ** block_levels(key_of[2], (ROWS,), ((0, 8),), -0.2, 0.2)), 0.049804688, 1.0).astype(jnp.bfloat16)
    node = plant(jax.random.randint(key_of[3], (ROWS,), 0, NODES), jax.random.fold_in(key_of[3], 1), 0, NODES - 1).astype(jnp.int32)
    return dict(bins=bins, grads=grads, hess=hess, node=node)


def reference(bins, grads, hess, node):
    stats = jnp.stack([grads.astype(jnp.float32), hess.astype(jnp.float32)], axis=1)

    def one_feature(column):
        labels = (node * BINS + column).astype(jnp.int32)
        summed = jax.ops.segment_sum(stats, labels, num_segments=NODES * BINS)
        return jnp.transpose(summed.reshape(NODES, BINS, 2), (2, 0, 1))

    hist = lax.map(one_feature, bins)
    totals = jax.ops.segment_sum(stats, node.astype(jnp.int32), num_segments=NODES)
    left = jnp.cumsum(hist, axis=3)
    grad_left = left[:, 0]
    hess_left = left[:, 1]
    grad_total = totals[:, 0][None, :, None]
    hess_total = totals[:, 1][None, :, None]
    gain = grad_left * grad_left / (hess_left + 1.0)
    gain = gain + (grad_total - grad_left) ** 2 / (hess_total - hess_left + 1.0)
    gain = gain - grad_total * grad_total / (hess_total + 1.0)
    best = jnp.max(gain, axis=(0, 2))
    return gain - best[None, :, None], best
```

```python
import functools
import jax
import jax.numpy as jnp
from jax import lax
from jax.experimental import pallas as pl
from jax.experimental.pallas import tpu as pltpu
from jax.sharding import PartitionSpec as P

BINS = 256
NODES = 8
LANES = 128
LOW = 64
TILE = 256
GROUP = TILE // LOW
HALVES = LANES // LOW
SLOTS = NODES * BINS // LANES


def hist_kernel(bins_ref, node_ref, g_ref, h_ref, out_ref, high_ref, low_ref, g_all, h_all, acc_ref):
    features, rows = bins_ref.shape

    @pl.when(pl.program_id(0) == 0)
    def _():
        g_all[...] = jnp.broadcast_to(g_ref[...], g_all.shape).astype(jnp.bfloat16)
        h_all[...] = jnp.broadcast_to(h_ref[...], h_all.shape).astype(jnp.bfloat16)

    bins = bins_ref[...]
    half = (bins // LOW) % HALVES
    slot = node_ref[...] * (BINS // LANES) + bins // LANES
    high_ref[...] = (half * SLOTS + slot).astype(jnp.float32)
    low_ref[...] = (bins % LOW).astype(jnp.float32)
    place = lax.broadcasted_iota(jnp.int32, (SLOTS, rows), 0).astype(jnp.bfloat16)
    zero = jnp.zeros((SLOTS, rows), jnp.bfloat16)
    one = jnp.ones((SLOTS, rows), jnp.bfloat16)
    for first in range(0, features, GROUP):
        left, right = [], []
        for f in range(first, first + GROUP):
            high = jnp.broadcast_to(high_ref[f : f + 1, :], (SLOTS, rows)).astype(jnp.bfloat16)
            low = jnp.broadcast_to(low_ref[f : f + 1, :], (SLOTS, rows)).astype(jnp.bfloat16)
            for j in range(HALVES):
                here = high == place + jnp.asarray(SLOTS * j, jnp.bfloat16)
                left += [jnp.where(here, g_all[...], zero), jnp.where(here, h_all[...], zero)]
            for j in range(LOW // SLOTS):
                here = low == place + jnp.asarray(SLOTS * j, jnp.bfloat16)
                right.append(jnp.where(here, one, zero))
        acc_ref[...] = lax.dot_general(
            jnp.concatenate(left, 0),
            jnp.concatenate(right, 0),
            (((1,), (1,)), ((), ())),
            preferred_element_type=jnp.float32,
        )
        for i in range(GROUP):
            parts = []
            for j in range(HALVES):
                top = (i * HALVES + j) * 2 * SLOTS
                parts.append(acc_ref[top : top + 2 * SLOTS, i * LOW : (i + 1) * LOW])
            out_ref[first + i] = jnp.concatenate(parts, 1)


def local_hist(bins, node, grads, hess, block):
    features, rows = bins.shape
    whole = pl.BlockSpec((1, rows), lambda i: (0, 0))
    return pl.pallas_call(
        hist_kernel,
        grid=(features // block,),
        in_specs=[pl.BlockSpec((block, rows), lambda i: (i, 0)), whole, whole, whole],
        out_specs=pl.BlockSpec((block, 2 * SLOTS, LANES), lambda i: (i, 0, 0)),
        out_shape=jax.ShapeDtypeStruct((features, 2 * SLOTS, LANES), jnp.float32),
        scratch_shapes=[
            pltpu.VMEM((block, rows), jnp.float32),
            pltpu.VMEM((block, rows), jnp.float32),
            pltpu.VMEM((SLOTS, rows), jnp.bfloat16),
            pltpu.VMEM((SLOTS, rows), jnp.bfloat16),
            pltpu.VMEM((GROUP * HALVES * 2 * SLOTS, TILE), jnp.float32),
        ],
        compiler_params=pltpu.CompilerParams(vmem_limit_bytes=56 << 20),
    )(bins, node, grads, hess)


def gain_kernel(hist_ref, gain_ref, best_ref):
    x = hist_ref[...]
    features = x.shape[0]
    x = x.reshape(features * 2 * SLOTS, LANES)
    lane = lax.broadcasted_iota(jnp.int32, x.shape, 1)
    step = 1
    while step < LANES:
        x = x + jnp.where(lane >= step, pltpu.roll(x, step, 1), 0.0)
        step *= 2
    row = lax.broadcasted_iota(jnp.int32, x.shape, 0)
    ends = jnp.broadcast_to(x[:, LANES - 1 :], x.shape)
    upper = row % 2 == 1
    n_rows = x.shape[0]
    left = x + jnp.where(upper, pltpu.roll(ends, 1, 0), 0.0)
    total = jnp.where(upper, pltpu.roll(ends, 1, 0), pltpu.roll(ends, n_rows - 1, 0)) + ends
    left = left.reshape(features, 2, SLOTS, LANES)
    total = total.reshape(features, 2, SLOTS, LANES)
    gl, hl = left[:, 0], left[:, 1]
    gt, ht = total[:, 0], total[:, 1]
    gain = gl * gl / (hl + 1.0)
    gain = gain + (gt - gl) ** 2 / (ht - hl + 1.0)
    gain = gain - gt * gt / (ht + 1.0)
    gain_ref[...] = gain
    best_ref[...] = jnp.max(gain, axis=0)


def per_device(bins, grads, hess, node):
    rows = bins.shape[1]
    g = grads.astype(jnp.float32).reshape(1, rows)
    h = hess.astype(jnp.float32).reshape(1, rows)
    part = local_hist(bins, node.reshape(1, rows), g, h, 8)
    hist = lax.psum_scatter(part, "row", scatter_dimension=0, tiled=True)
    features = hist.shape[0]
    gain, top = pl.pallas_call(
        gain_kernel,
        out_shape=(
            jax.ShapeDtypeStruct((features, SLOTS, LANES), jnp.float32),
            jax.ShapeDtypeStruct((SLOTS, LANES), jnp.float32),
        ),
    )(hist)
    local_best = jnp.max(top.reshape(NODES, BINS // LANES * LANES), axis=1)
    best = lax.pmax(local_best, ("row", "feat"))
    out = gain.reshape(features, NODES, BINS) - best[None, :, None]
    return out, best


def solution(mesh):
    return jax.shard_map(
        per_device,
        mesh=mesh,
        in_specs=(P("feat", "row"), P("row"), P("row"), P("row")),
        out_specs=(P(("feat", "row"), None, None), P()),
        check_vma=False,
    )
```

```python
import functools
import jax
import jax.numpy as jnp
from jax import lax
from jax.experimental import pallas as pl
from jax.experimental.pallas import tpu as pltpu
from jax.sharding import PartitionSpec as P

BINS = 256
NODES = 8
LANES = 128
SUBLANES = 8
LOW = 64
TILE = 256
GROUP = TILE // LOW
HALVES = LANES // LOW
TOPS = BINS // LANES
SLOTS = NODES * TOPS
LINES = 2 * SLOTS
MESH = pl.DeviceIdType.MESH


def partner(me, k, n):
    if n & (n - 1):
        return (me + k) % n
    out, weight = 0, 1
    while weight < n:
        out = out + (((me // weight) % 2 + (k // weight) % 2) % 2) * weight
        weight *= 2
    return out


def kernel(
    n, m, block, chunks, bins_hbm, node_ref, g_ref, h_ref, out_ref, best_ref,
    bins_buf, high_ref, low_ref, g_all, h_all, acc_ref, stage, landed, row_best, feat_best,
    load_sem, send_sem, recv_sem, row_send, row_recv, feat_send, feat_recv,
):
    rows = bins_buf.shape[2]
    me = lax.axis_index("row")
    mine = lax.axis_index("feat")
    steps = n * chunks
    sent = (n - 1) * chunks

    def place_of(s):
        return (partner(me, n - 1 - s // chunks, n) * chunks + s % chunks) * block

    def load(s):
        start = pl.multiple_of((place_of(s) // SUBLANES) * SUBLANES, SUBLANES)
        return pltpu.make_async_copy(
            bins_hbm.at[pl.ds(start, SUBLANES), :], bins_buf.at[s % 2], load_sem.at[s % 2]
        )

    def send(s):
        k = n - 1 - s // chunks
        return pltpu.make_async_remote_copy(
            src_ref=stage.at[s],
            dst_ref=landed.at[s],
            send_sem=send_sem.at[s],
            recv_sem=recv_sem.at[s],
            device_id={"row": partner(me, k, n)},
            device_id_type=MESH,
        )

    load(0).start()
    barrier = pltpu.get_barrier_semaphore()
    for k in range(1, n):
        pl.semaphore_signal(barrier, inc=1, device_id={"row": (me + k) % n}, device_id_type=MESH)
    for k in range(1, m):
        pl.semaphore_signal(barrier, inc=1, device_id={"feat": (mine + k) % m}, device_id_type=MESH)

    g = g_ref[...].astype(jnp.float32)
    h = h_ref[...].astype(jnp.float32)
    for i in range(rows // LANES):
        cols = slice(i * LANES, (i + 1) * LANES)
        g_all[:, cols] = jnp.broadcast_to(g[i : i + 1, :], (SLOTS, LANES)).astype(jnp.bfloat16)
        h_all[:, cols] = jnp.broadcast_to(h[i : i + 1, :], (SLOTS, LANES)).astype(jnp.bfloat16)
    pl.semaphore_wait(barrier, n + m - 2)

    def step(s, carry):
        load(s).wait()

        @pl.when(s + 1 < steps)
        def _():
            load(s + 1).start()

        @pl.when((s >= 1) & (s <= sent))
        def _():
            send(s - 1).start()

        offset = 0 if block % SUBLANES == 0 else place_of(s) % SUBLANES
        bins = bins_buf[s % 2]
        half = (bins // LOW) % HALVES
        slot = (bins // LANES) * NODES + node_ref[...]
        high_ref[...] = (half * SLOTS + slot).astype(jnp.float32)
        low_ref[...] = (bins % LOW).astype(jnp.float32)
        place = lax.broadcasted_iota(jnp.int32, (SLOTS, rows), 0).astype(jnp.bfloat16)
        zero = jnp.zeros((SLOTS, rows), jnp.bfloat16)
        one = jnp.ones((SLOTS, rows), jnp.bfloat16)
        for first in range(0, block, GROUP):
            left, right = [], []
            for f in range(first, first + GROUP):
                row = pl.ds(offset + f, 1)
                high = jnp.broadcast_to(high_ref[row, :], (SLOTS, rows)).astype(jnp.bfloat16)
                low = jnp.broadcast_to(low_ref[row, :], (SLOTS, rows)).astype(jnp.bfloat16)
                for j in range(HALVES):
                    here = high == place + jnp.asarray(SLOTS * j, jnp.bfloat16)
                    left += [jnp.where(here, g_all[...], zero), jnp.where(here, h_all[...], zero)]
                for j in range(LOW // SLOTS):
                    here = low == place + jnp.asarray(SLOTS * j, jnp.bfloat16)
                    right.append(jnp.where(here, one, zero))
            acc_ref[...] = lax.dot_general(
                jnp.concatenate(left, 0),
                jnp.concatenate(right, 0),
                (((1,), (1,)), ((), ())),
                preferred_element_type=jnp.float32,
            )
            for i in range(GROUP):
                parts = []
                for j in range(HALVES):
                    top = (i * HALVES + j) * LINES
                    parts.append(acc_ref[top : top + LINES, i * LOW : (i + 1) * LOW])
                stage[s, first + i] = jnp.concatenate(parts, 1)
        return carry

    lax.fori_loop(0, steps, step, 0)

    def drain(s, carry):
        send(s).wait()
        return carry

    lax.fori_loop(0, sent, drain, 0)

    lane = lax.broadcasted_iota(jnp.int32, (block * 2 * TOPS * NODES, LANES), 1)

    def finish(c, top_gain):
        def add(k, total):
            return total + landed[k * chunks + c]

        x = lax.fori_loop(0, n - 1, add, stage[sent + c])
        x = x.reshape(block * LINES, LANES)
        shift = 1
        while shift < LANES:
            x = x + jnp.where(lane >= shift, pltpu.roll(x, shift, 1), 0.0)
            shift *= 2
        x = x.reshape(block, 2, TOPS, NODES, LANES)
        left, total = [], jnp.zeros((block, 2, NODES, LANES), jnp.float32)
        for t in range(TOPS):
            left.append(x[:, :, t] + total)
            total = total + jnp.broadcast_to(x[:, :, t, :, LANES - 1 :], total.shape)
        gt, ht = total[:, 0], total[:, 1]
        base = gt * gt / (ht + 1.0)
        for t in range(TOPS):
            gl, hl = left[t][:, 0], left[t][:, 1]
            gain = gl * gl / (hl + 1.0)
            gain = gain + (gt - gl) * (gt - gl) / (ht - hl + 1.0)
            gain = gain - base
            out_ref[pl.ds(c * block, block), :, t * LANES : (t + 1) * LANES] = gain
            top_gain = jnp.maximum(top_gain, jnp.max(gain, axis=0))
        return top_gain

    top_gain = lax.fori_loop(0, chunks, finish, jnp.full((NODES, LANES), -jnp.inf, jnp.float32))

    def exchange(value, slots, count, axis, index, sems, arrived):
        slots[0] = jnp.broadcast_to(jnp.max(value, axis=1, keepdims=True), (NODES, LANES))
        copies = []
        for k in range(1, count):
            copies.append(
                pltpu.make_async_remote_copy(
                    src_ref=slots.at[0],
                    dst_ref=slots.at[k],
                    send_sem=sems.at[k - 1],
                    recv_sem=arrived.at[k - 1],
                    device_id={axis: (index + k) % count},
                    device_id_type=MESH,
                )
            )
            copies[-1].start()
        for copy in copies:
            copy.wait()
        best = slots[0]
        for k in range(1, count):
            best = jnp.maximum(best, slots[k])
        return best

    best = exchange(top_gain, row_best, n, "row", me, row_send, row_recv)
    best = exchange(best, feat_best, m, "feat", mine, feat_send, feat_recv)
    best_ref[...] = best
    for t in range(TOPS):
        cols = slice(t * LANES, (t + 1) * LANES)
        out_ref[:, :, cols] = out_ref[:, :, cols] - best[None]


def solution(mesh):
    n, m = mesh.shape["row"], mesh.shape["feat"]

    def per_device(bins, grads, hess, node):
        features, rows = bins.shape
        own = features // n
        block = min(own, SUBLANES)
        chunks = own // block
        vmem = pl.BlockSpec(memory_space=pltpu.VMEM)
        piece = (block, LINES, LANES)
        out, best = pl.pallas_call(
            functools.partial(kernel, n, m, block, chunks),
            in_specs=[pl.BlockSpec(memory_space=pl.ANY), vmem, vmem, vmem],
            out_specs=(vmem, vmem),
            out_shape=(
                jax.ShapeDtypeStruct((own, NODES, BINS), jnp.float32),
                jax.ShapeDtypeStruct((NODES, LANES), jnp.float32),
            ),
            scratch_shapes=[
                pltpu.VMEM((2, SUBLANES, rows), jnp.int32),
                pltpu.VMEM((SUBLANES, rows), jnp.float32),
                pltpu.VMEM((SUBLANES, rows), jnp.float32),
                pltpu.VMEM((SLOTS, rows), jnp.bfloat16),
                pltpu.VMEM((SLOTS, rows), jnp.bfloat16),
                pltpu.VMEM((GROUP * HALVES * LINES, TILE), jnp.float32),
                pltpu.VMEM((n * chunks,) + piece, jnp.float32),
                pltpu.VMEM(((n - 1) * chunks,) + piece, jnp.float32),
                pltpu.VMEM((n, NODES, LANES), jnp.float32),
                pltpu.VMEM((m, NODES, LANES), jnp.float32),
                pltpu.SemaphoreType.DMA((2,)),
                pltpu.SemaphoreType.DMA(((n - 1) * chunks,)),
                pltpu.SemaphoreType.DMA(((n - 1) * chunks,)),
                pltpu.SemaphoreType.DMA((n - 1,)),
                pltpu.SemaphoreType.DMA((n - 1,)),
                pltpu.SemaphoreType.DMA((m - 1,)),
                pltpu.SemaphoreType.DMA((m - 1,)),
            ],
            compiler_params=pltpu.CompilerParams(
                collective_id=0, has_side_effects=True, vmem_limit_bytes=56 << 20
            ),
        )(bins, node.reshape(1, rows), grads.reshape(-1, LANES), hess.reshape(-1, LANES))
        return out, best[:, 0]

    return jax.shard_map(
        per_device,
        mesh=mesh,
        in_specs=(P("feat", "row"), P("row"), P("row"), P("row")),
        out_specs=(P(("feat", "row"), None, None), P()),
        check_vma=False,
    )
```

```python
import functools
import jax
import jax.numpy as jnp
from jax import lax
from jax.experimental import pallas as pl
from jax.experimental.pallas import tpu as pltpu
from jax.sharding import PartitionSpec as P

BINS = 256
NODES = 8
LANES = 128
SUBLANES = 8
LOW = 64
TILE = 256
GROUP = TILE // LOW
HALVES = LANES // LOW
TOPS = BINS // LANES
SLOTS = NODES * TOPS
LINES = 2 * SLOTS
MESH = pl.DeviceIdType.MESH


def partner(me, k, n):
    if n & (n - 1):
        return (me + k) % n
    out, weight = 0, 1
    while weight < n:
        out = out + (((me // weight) % 2 + (k // weight) % 2) % 2) * weight
        weight *= 2
    return out


def kernel(
    n, m, block, chunks, bins_hbm, node_ref, g_ref, h_ref, out_ref, best_ref,
    bins_buf, high_ref, low_ref, g_all, h_all, acc_ref, stage, landed, row_best, feat_best,
    load_sem, send_sem, recv_sem, row_send, row_recv, feat_send, feat_recv,
):
    rows = bins_buf.shape[2]
    me = lax.axis_index("row")
    mine = lax.axis_index("feat")
    steps = n * chunks
    sent = (n - 1) * chunks

    def place_of(s):
        return (partner(me, n - 1 - s // chunks, n) * chunks + s % chunks) * block

    def load(s):
        start = pl.multiple_of((place_of(s) // SUBLANES) * SUBLANES, SUBLANES)
        return pltpu.make_async_copy(
            bins_hbm.at[pl.ds(start, bins_buf.shape[1]), :], bins_buf.at[s % 2], load_sem.at[s % 2]
        )

    def send(s):
        k = n - 1 - s // chunks
        return pltpu.make_async_remote_copy(
            src_ref=stage.at[s],
            dst_ref=landed.at[s],
            send_sem=send_sem.at[s],
            recv_sem=recv_sem.at[s],
            device_id={"row": partner(me, k, n)},
            device_id_type=MESH,
        )

    load(0).start()
    barrier = pltpu.get_barrier_semaphore()
    for k in range(1, n):
        pl.semaphore_signal(barrier, inc=1, device_id={"row": (me + k) % n}, device_id_type=MESH)
    for k in range(1, m):
        pl.semaphore_signal(barrier, inc=1, device_id={"feat": (mine + k) % m}, device_id_type=MESH)

    g = g_ref[...].astype(jnp.float32)
    h = h_ref[...].astype(jnp.float32)
    for i in range(rows // LANES):
        cols = slice(i * LANES, (i + 1) * LANES)
        g_all[:, cols] = jnp.broadcast_to(g[i : i + 1, :], (SLOTS, LANES)).astype(jnp.bfloat16)
        h_all[:, cols] = jnp.broadcast_to(h[i : i + 1, :], (SLOTS, LANES)).astype(jnp.bfloat16)
    pl.semaphore_wait(barrier, n + m - 2)

    def step(s, carry):
        load(s).wait()

        @pl.when(s + 1 < steps)
        def _():
            load(s + 1).start()

        @pl.when((s >= 1) & (s <= sent))
        def _():
            send(s - 1).start()

        offset = 0 if block % SUBLANES == 0 else place_of(s) % SUBLANES
        bins = bins_buf[s % 2]
        upper = bins >= LANES
        rest = jnp.where(upper, bins - LANES, bins)
        second = rest >= LOW
        slot = node_ref[...] + jnp.where(upper, NODES, 0)
        high_ref[...] = jnp.where(second, slot + SLOTS, slot).astype(jnp.float32)
        low_ref[...] = jnp.where(second, rest - LOW, rest).astype(jnp.float32)
        place = lax.broadcasted_iota(jnp.int32, (SLOTS, rows), 0).astype(jnp.bfloat16)
        zero = jnp.zeros((SLOTS, rows), jnp.bfloat16)
        one = jnp.ones((SLOTS, rows), jnp.bfloat16)
        for first in range(0, block, GROUP):
            left, right = [], []
            for f in range(first, first + GROUP):
                row = pl.ds(offset + f, 1)
                high = jnp.broadcast_to(high_ref[row, :], (SLOTS, rows)).astype(jnp.bfloat16)
                low = jnp.broadcast_to(low_ref[row, :], (SLOTS, rows)).astype(jnp.bfloat16)
                for j in range(HALVES):
                    here = high == place + jnp.asarray(SLOTS * j, jnp.bfloat16)
                    left += [jnp.where(here, g_all[...], zero), jnp.where(here, h_all[...], zero)]
                for j in range(LOW // SLOTS):
                    here = low == place + jnp.asarray(SLOTS * j, jnp.bfloat16)
                    right.append(jnp.where(here, one, zero))
            acc_ref[...] = lax.dot_general(
                jnp.concatenate(left, 0),
                jnp.concatenate(right, 0),
                (((1,), (1,)), ((), ())),
                preferred_element_type=jnp.float32,
            )
            for i in range(GROUP):
                parts = []
                for j in range(HALVES):
                    top = (i * HALVES + j) * LINES
                    parts.append(acc_ref[top : top + LINES, i * LOW : (i + 1) * LOW])
                stage[s, first + i] = jnp.concatenate(parts, 1)
        return carry

    lax.fori_loop(0, steps, step, 0)

    def drain(s, carry):
        send(s).wait()
        return carry

    lax.fori_loop(0, sent, drain, 0)

    lane = lax.broadcasted_iota(jnp.int32, (block * 2 * TOPS * NODES, LANES), 1)

    def finish(c, top_gain):
        def add(k, total):
            return total + landed[k * chunks + c]

        x = lax.fori_loop(0, n - 1, add, stage[sent + c])
        x = x.reshape(block * LINES, LANES)
        shift = 1
        while shift < LANES:
            x = x + jnp.where(lane >= shift, pltpu.roll(x, shift, 1), 0.0)
            shift *= 2
        x = x.reshape(block, 2, TOPS, NODES, LANES)
        left, total = [], jnp.zeros((block, 2, NODES, LANES), jnp.float32)
        for t in range(TOPS):
            left.append(x[:, :, t] + total)
            total = total + jnp.broadcast_to(x[:, :, t, :, LANES - 1 :], total.shape)
        gt, ht = total[:, 0], total[:, 1]
        base = gt * gt / (ht + 1.0)
        for t in range(TOPS):
            gl, hl = left[t][:, 0], left[t][:, 1]
            gain = gl * gl / (hl + 1.0)
            gain = gain + (gt - gl) * (gt - gl) / (ht - hl + 1.0)
            gain = gain - base
            out_ref[pl.ds(c * block, block), :, t * LANES : (t + 1) * LANES] = gain
            top_gain = jnp.maximum(top_gain, jnp.max(gain, axis=0))
        return top_gain

    top_gain = lax.fori_loop(0, chunks, finish, jnp.full((NODES, LANES), -jnp.inf, jnp.float32))

    def exchange(value, slots, count, axis, index, sems, arrived):
        slots[0] = jnp.broadcast_to(jnp.max(value, axis=1, keepdims=True), (NODES, LANES))
        copies = []
        for k in range(1, count):
            copies.append(
                pltpu.make_async_remote_copy(
                    src_ref=slots.at[0],
                    dst_ref=slots.at[k],
                    send_sem=sems.at[k - 1],
                    recv_sem=arrived.at[k - 1],
                    device_id={axis: (index + k) % count},
                    device_id_type=MESH,
                )
            )
            copies[-1].start()
        for copy in copies:
            copy.wait()
        best = slots[0]
        for k in range(1, count):
            best = jnp.maximum(best, slots[k])
        return best

    best = exchange(top_gain, row_best, n, "row", me, row_send, row_recv)
    best = exchange(best, feat_best, m, "feat", mine, feat_send, feat_recv)
    across = lax.broadcasted_iota(jnp.int32, (NODES, LANES), 1)
    down = lax.broadcasted_iota(jnp.int32, (NODES, LANES), 0)
    flat = jnp.max(jnp.where(across == down, best, -jnp.inf), axis=0, keepdims=True)
    best_ref[...] = flat[:, :NODES]


def solution(mesh):
    n, m = mesh.shape["row"], mesh.shape["feat"]

    def per_device(bins, grads, hess, node):
        features, rows = bins.shape
        own = features // n
        block = own if own < SUBLANES else next(b for b in (2 * SUBLANES, SUBLANES) if own % b == 0)
        held = max(block, SUBLANES)
        chunks = own // block
        vmem = pl.BlockSpec(memory_space=pltpu.VMEM)
        piece = (block, LINES, LANES)
        out, best = pl.pallas_call(
            functools.partial(kernel, n, m, block, chunks),
            in_specs=[pl.BlockSpec(memory_space=pl.ANY), vmem, vmem, vmem],
            out_specs=(vmem, vmem),
            out_shape=(
                jax.ShapeDtypeStruct((own, NODES, BINS), jnp.float32),
                jax.ShapeDtypeStruct((1, NODES), jnp.float32),
            ),
            scratch_shapes=[
                pltpu.VMEM((2, held, rows), jnp.int32),
                pltpu.VMEM((held, rows), jnp.float32),
                pltpu.VMEM((held, rows), jnp.float32),
                pltpu.VMEM((SLOTS, rows), jnp.bfloat16),
                pltpu.VMEM((SLOTS, rows), jnp.bfloat16),
                pltpu.VMEM((GROUP * HALVES * LINES, TILE), jnp.float32),
                pltpu.VMEM((n * chunks,) + piece, jnp.float32),
                pltpu.VMEM(((n - 1) * chunks,) + piece, jnp.float32),
                pltpu.VMEM((n, NODES, LANES), jnp.float32),
                pltpu.VMEM((m, NODES, LANES), jnp.float32),
                pltpu.SemaphoreType.DMA((2,)),
                pltpu.SemaphoreType.DMA(((n - 1) * chunks,)),
                pltpu.SemaphoreType.DMA(((n - 1) * chunks,)),
                pltpu.SemaphoreType.DMA((n - 1,)),
                pltpu.SemaphoreType.DMA((n - 1,)),
                pltpu.SemaphoreType.DMA((m - 1,)),
                pltpu.SemaphoreType.DMA((m - 1,)),
            ],
            compiler_params=pltpu.CompilerParams(
                collective_id=0, has_side_effects=True, vmem_limit_bytes=56 << 20
            ),
        )(bins, node.reshape(1, rows), grads.reshape(-1, LANES), hess.reshape(-1, LANES))
        best = best.reshape(NODES)
        return out - best[None, :, None], best

    return jax.shard_map(
        per_device,
        mesh=mesh,
        in_specs=(P("feat", "row"), P("row"), P("row"), P("row")),
        out_specs=(P(("feat", "row"), None, None), P()),
        check_vma=False,
    )
```
